32 devices in a mesh: row: 8 (over y, x, core), col: 4 (over z).
Axes of the slice: x: 2, y: 2, z: 4, core: 2. Of those that a mesh axis runs over, the one named last changes fastest.
Arguments:
- positions: float32 [3, 32768], P(None, ('row', 'col')), may hold values from 0 to 1
- segments: float32 [3, 32768], P(None, ('row', 'col')), may hold values from -1.2 to 1.2
- radius: float32 [32768], P(('row', 'col')), may hold values from 0.05 to 0.2
- currents: float32 [2, 32768], P(None, ('row', 'col')), may hold values from -6 to 6
- resist: float32 [32768], P(('row', 'col')), may hold values from 0.3 to 3
- slot_of: int32 [32768], P(('row', 'col')), may hold values from 0 to 1023, as said below
- pair_list: int32 [1024, 2], P(('row', 'col')), may hold values from 0 to 63, as said below
- near_flag: int32 [1024], P(('row', 'col')), may hold values from 0 to 2, as said below
Outputs:
- voltage: float32 [2, 32768], P(None, ('row', 'col'))
The draws below stay inside these ranges and needn't reach their ends.
Inputs may be any that keep to these rules, and one draw needn't show every extreme that they name: `slot_of`: the elements of shard d hold the values 0 to 1023 once each; a value s puts the element in cluster d * 2 + s // 512. `pair_list`: shard d = r * 4 + c lists 32 slots; each live slot holds a pair (I, J) with I <= J, I in clusters r * 2 * 4 to (r + 1) * 2 * 4 - 1 and (J // 2) % 4 = c; a pair stands in one live slot at most, over all shards. Empty slots hold I = r * 2 * 4 and J = c * 2. `near_flag`: 0 marks an empty slot.
All inputs are finite; a program needn't handle non-finite values.
Results may differ from the reference program's by a relative error of at most 0.0003.
Values sent between devices are 32-bit elements; how exact they have to be, the bound alone decides.
A program may use at most 64 MiB of HBM per device.

```python
import math
import jax
import jax.numpy as jnp
from jax import lax

CS = 512
CPD = 2
PCAP = 32
NE = 32768
N_ROW = 8
N_COL = 4
DEVICES = 32


def list_layout(key):
    base_key = jax.random.fold_in(key, 7177)
    row_span = CPD * N_COL
    col_span = CPD * N_ROW
    square = row_span * col_span
    device_keys = jax.random.split(base_key, DEVICES)

    def one_device(device_id, device_key):
        row_pos = device_id // N_COL
        col_pos = device_id % N_COL
        candidate = jnp.arange(square, dtype=jnp.int32)
        first_local = candidate // col_span
        second_local = candidate % col_span
        first_id = row_pos * row_span + first_local
        second_id = (second_local // CPD * N_COL + col_pos) * CPD + second_local % CPD
        allowed = second_id >= first_id
        allowed_count = jnp.sum(allowed.astype(jnp.int32))
        key_order, key_jitter, key_near, key_shuffle = jax.random.split(device_key, 4)
        priority = jax.random.permutation(key_order, square).astype(jnp.int32)
        scores = jnp.where(allowed, priority + square, priority)
        _, chosen = lax.top_k(scores, PCAP)
        jitter = jax.random.randint(key_jitter, (), 0, PCAP // 4 + 1)
        wanted = PCAP * (N_ROW - row_pos) // N_ROW - jnp.where(row_pos > 0, jitter, 0)
        live_count = jnp.minimum(allowed_count, jnp.maximum(wanted, 1))
        slot_index = jnp.arange(PCAP, dtype=jnp.int32)
        is_live = slot_index < live_count
        pick_first = jnp.where(is_live, first_id[chosen], row_pos * row_span)
        pick_second = jnp.where(is_live, second_id[chosen], col_pos * CPD)
        near_roll = jax.random.randint(key_near, (PCAP,), 0, 8)
        is_close = pick_second - pick_first < 2 * row_span
        is_near = jnp.where(is_close, near_roll < 4, near_roll < 1)
        flags = jnp.where(is_live, jnp.where(is_near, 2, 1), 0).astype(jnp.int32)
        shuffle = jax.random.permutation(key_shuffle, PCAP)
        pairs = jnp.stack([pick_first, pick_second], 1).astype(jnp.int32)
        return (pairs[shuffle], flags[shuffle])
    pairs, flags = jax.vmap(one_device)(jnp.arange(DEVICES, dtype=jnp.int32), device_keys)
    return (pairs.reshape(DEVICES * PCAP, 2), flags.reshape(DEVICES * PCAP))


def draw_pair_list(key, part):
    pairs, _ = list_layout(key)
    return pairs


def draw_near_flag(key, part):
    _, flags = list_layout(key)
    return flags


def draw_slot_of(key, part):
    per_device = CPD * CS
    device_keys = jax.random.split(jax.random.fold_in(key, 3301), DEVICES)

    def one_device(device_key):
        return jax.random.permutation(device_key, per_device)
    return jax.vmap(one_device)(device_keys).reshape(-1).astype(jnp.int32)


def level_of(stream_key, extent, shards, smallest, top_value):
    def one(dim, shards_of):
        steps = jax.random.uniform(jax.random.fold_in(jax.random.fold_in(stream_key, 6), dim), (shards_of,), jnp.float32, smallest / len(shards), top_value / len(shards))
        return jnp.repeat(jnp.exp(steps), extent[dim] // shards_of).reshape((-1,) + (1,) * (len(extent) - dim - 1))

    factor_of = one(*shards[0])
    for cut in shards[1:]:
        factor_of = factor_of * one(*cut)
    return factor_of


def noise(stream_key, extent, scale, limit, shards=(), kind=jnp.bfloat16):
    gain = level_of(stream_key, extent, shards, -0.22, 0.18) if shards else 1.0
    values = jax.random.normal(stream_key, extent, jnp.float32) * scale * gain
    return jnp.minimum(jnp.maximum(values, -limit), limit).astype(kind)


def setup_inputs(seed: int = 0) -> dict:
    arg_keys = jax.random.split(jax.random.key(seed), 9)
    positions = jnp.clip(1.0 * jax.random.uniform(arg_keys[0], (3, NE), jnp.float32) ** level_of(arg_keys[0], (3, NE), ((1, 32),), -0.2, 0.2), 0.0, 1.0)
    segments = noise(arg_keys[1], (3, NE), 0.2, 1.2, ((1, 32),), jnp.float32)
    radius = jnp.clip(jnp.exp(math.log(0.2) - 1.3862944 * jax.random.uniform(arg_keys[2], (NE,), jnp.float32) ** level_of(arg_keys[2], (NE,), ((0, 32),), -0.2, 0.2)), 0.05, 0.2)
    currents = noise(arg_keys[3], (2, NE), 1.0, 6.0, ((1, 32),), jnp.float32)
    resist = jnp.clip(jnp.exp(math.log(3.0) - 2.3025851 * jax.random.uniform(arg_keys[4], (NE,), jnp.float32) ** level_of(arg_keys[4], (NE,), ((0, 32),), -0.2, 0.2)), 0.3, 3.0)
    slot_of = draw_slot_of(jax.random.fold_in(arg_keys[8], 71), 0)
    pair_list = draw_pair_list(jax.random.fold_in(arg_keys[8], 71), 0)
    near_flag = draw_near_flag(jax.random.fold_in(arg_keys[8], 71), 0)
    return dict(positions=positions, segments=segments, radius=radius, currents=currents, resist=resist, slot_of=slot_of, pair_list=pair_list, near_flag=near_flag)


gauss_step = 0.5 / math.sqrt(3.0)
kernel_gain = 0.25

def tile_block(points_first, vectors_first, radii_first, points_second, vectors_second, radii_second, is_near):
    softening = radii_first[:, None] ** 2 + radii_second[None, :] ** 2
    alignment = vectors_first[0][:, None] * vectors_second[0][None, :]
    for component in (1, 2):
        alignment = alignment + vectors_first[component][:, None] * vectors_second[component][None, :]

    def far_part():
        squared = softening
        for component in range(3):
            squared = squared + (points_first[component][:, None] - points_second[component][None, :]) ** 2
        return 1.0 / jnp.sqrt(squared)

    def near_part():
        summed = jnp.zeros_like(softening)
        for sign_first in (-1.0, 1.0):
            for sign_second in (-1.0, 1.0):
                squared = softening
                for component in range(3):
                    moved_first = points_first[component] + sign_first * gauss_step * vectors_first[component]
                    moved_second = points_second[component] + sign_second * gauss_step * vectors_second[component]
                    squared = squared + (moved_first[:, None] - moved_second[None, :]) ** 2
                summed = summed + 1.0 / jnp.sqrt(squared)
        return 0.25 * summed
    inverse = lax.cond(is_near, near_part, far_part)
    return kernel_gain * alignment * inverse

def reference(positions, segments, radius, currents, resist, slot_of, pair_list, near_flag):
    per_device = CPD * CS
    device_of = jnp.arange(NE, dtype=jnp.int32) // per_device
    global_slot = (device_of * per_device + slot_of).astype(jnp.int32)
    packed = jnp.concatenate([positions, segments, radius[None, :], currents], 0)
    ordered = jnp.zeros_like(packed).at[:, global_slot].set(packed)

    def advance(induced_sum, slot_entry):
        pair_entry, flag_value = slot_entry
        first_id = pair_entry[0].astype(jnp.int32)
        second_id = pair_entry[1].astype(jnp.int32)
        block_first = lax.dynamic_slice_in_dim(ordered, first_id * CS, CS, 1)
        block_second = lax.dynamic_slice_in_dim(ordered, second_id * CS, CS, 1)
        kernel_tile = tile_block(block_first[0:3], block_first[3:6], block_first[6], block_second[0:3], block_second[3:6], block_second[6], flag_value == 2)
        weight_live = (flag_value > 0).astype(induced_sum.dtype)
        weight_mirror = weight_live * (first_id != second_id).astype(induced_sum.dtype)
        direct_part = weight_live * jnp.dot(block_second[7:9], kernel_tile.T, precision=lax.Precision.HIGHEST)
        mirror_part = weight_mirror * jnp.dot(block_first[7:9], kernel_tile, precision=lax.Precision.HIGHEST)
        current = lax.dynamic_slice_in_dim(induced_sum, first_id * CS, CS, 1)
        induced_sum = lax.dynamic_update_slice_in_dim(induced_sum, current + direct_part, first_id * CS, 1)
        current = lax.dynamic_slice_in_dim(induced_sum, second_id * CS, CS, 1)
        induced_sum = lax.dynamic_update_slice_in_dim(induced_sum, current + mirror_part, second_id * CS, 1)
        return (induced_sum, None)
    start_sum = jnp.zeros((2, NE), packed.dtype)
    induced_field, _ = lax.scan(advance, start_sum, (pair_list, near_flag))
    induced = induced_field[:, global_slot]
    voltage_real = resist * currents[0] - induced[1]
    voltage_imag = resist * currents[1] + induced[0]
    return jnp.stack([voltage_real, voltage_imag])
```

```python
import functools
import math

import jax
import jax.numpy as jnp
from jax import lax
from jax.experimental import pallas as pl
from jax.experimental.pallas import tpu as pltpu
from jax.sharding import PartitionSpec as P

CS = 512
F32 = jnp.float32
BF16 = jnp.bfloat16
MESH = pl.DeviceIdType.MESH
gauss_step = 0.5 / math.sqrt(3.0)
kernel_gain = 0.25
VMEM = pl.BlockSpec(memory_space=pltpu.VMEM)
CHUNK = 256


def split_three(value):
    high = value.astype(BF16).astype(F32)
    rest = value - high
    middle = rest.astype(BF16).astype(F32)
    return high, middle, rest - middle


def dot_nn(left, right):
    return lax.dot_general(left, right, (((1,), (0,)), ((), ())), preferred_element_type=F32)


def dot_nt(left, right):
    return lax.dot_general(left, right, (((1,), (1,)), ((), ())), preferred_element_type=F32)


def one_hot_rows(slots, start, count):
    rows = lax.broadcasted_iota(jnp.int32, (count, slots.shape[1]), 0) + start
    return jnp.where(rows == slots, 1.0, 0.0).astype(BF16)


def order_kernel(pos, seg, rad, cur, slot, pair, flag, main, extra, stack):
    clusters = main.shape[0]
    slots = slot[...]
    stack[...] = jnp.zeros_like(stack)
    for source, row in ((pos, 0), (seg, 3), (rad, 6), (cur, 7)):
        count = source.shape[0]
        for part, piece in enumerate(split_three(source[...])):
            stack[part * 16 + row : part * 16 + row + count, :] = piece
    parts = stack[...].astype(BF16)
    for cluster in range(clusters):
        sums = dot_nt(parts, one_hot_rows(slots, cluster * CS, CS))
        ordered = sums[0:16] + sums[16:32] + sums[32:48]
        main[cluster] = ordered[0:8]
        extra[cluster : cluster + 1, :] = ordered[8:9]
    listed = pair.shape[1]
    extra[clusters : clusters + 2, :] = jnp.zeros((2, CS), F32)
    extra[clusters : clusters + 1, 0:listed] = pair[0:1, :].astype(F32)
    extra[clusters : clusters + 1, 128 : 128 + listed] = pair[1:2, :].astype(F32)
    extra[clusters : clusters + 1, 256 : 256 + listed] = flag[...].astype(F32)


def order_elements(positions, segments, radius, currents, slot_of, pair_list, near_flag):
    local = positions.shape[1]
    clusters = local // CS
    return pl.pallas_call(
        order_kernel,
        out_shape=(
            jax.ShapeDtypeStruct((clusters, 8, CS), F32),
            jax.ShapeDtypeStruct((clusters + 2, CS), F32),
        ),
        in_specs=[VMEM] * 7,
        out_specs=(VMEM, VMEM),
        scratch_shapes=[pltpu.VMEM((48, local), F32)],
    )(
        positions,
        segments,
        radius[None, :],
        currents,
        slot_of[None, :],
        pair_list.T,
        near_flag[None, :],
    )


def pair_kernel(main, extra, total, feat_first, feat_second, weight_first, weight_second):
    devices, clusters = main.shape[0], main.shape[1]
    me = lax.axis_index("row") * lax.axis_size("col") + lax.axis_index("col")
    total[...] = jnp.zeros_like(total)
    for feat, ones in ((feat_first, 21), (feat_second, 18)):
        feat[...] = jnp.zeros_like(feat)
        for sign in range(2):
            feat[sign, ones : ones + 3, :] = jnp.ones((3, CS), F32)
    weight_first[...] = jnp.zeros_like(weight_first)
    weight_second[...] = jnp.zeros_like(weight_second)

    lists = extra[:, clusters, :]
    first_ids, second_ids, flags = lists[:, 0:128], lists[:, 128:256], lists[:, 256:384]
    code = (first_ids * 1024.0 + second_ids) * 4.0 + flags
    is_near = jnp.where(flags > 1.5, 1.0, 0.0)
    is_far = jnp.where(jnp.abs(flags - 1.0) < 0.5, 1.0, 0.0)
    before_lane = jnp.where(
        lax.broadcasted_iota(jnp.int32, (128, 128), 0) < lax.broadcasted_iota(jnp.int32, (128, 128), 1),
        1.0,
        0.0,
    ).astype(BF16)
    before_row = jnp.where(
        lax.broadcasted_iota(jnp.int32, (devices, devices), 1)
        < lax.broadcasted_iota(jnp.int32, (devices, devices), 0),
        1.0,
        0.0,
    ).astype(BF16)

    def rank_in(mask):
        in_row = dot_nn(mask.astype(BF16), before_lane)
        above = jnp.sum(dot_nn(before_row, mask.astype(BF16)), axis=1, keepdims=True)
        return in_row + above

    near_count = jnp.sum(is_near)
    live_count = near_count + jnp.sum(is_far)
    rank = jnp.where(
        is_near > 0.5,
        rank_in(is_near),
        jnp.where(is_far > 0.5, rank_in(is_far) + near_count, -1.0),
    ).astype(jnp.int32)
    mine = (live_count.astype(jnp.int32) + (devices - 1 - me)) // devices

    def pick(turn):
        found = jnp.where(rank == turn * devices + me, code, 0.0)
        return jnp.sum(found).astype(jnp.int32)

    def load(cluster, weights):
        device, local = cluster // clusters, cluster % clusters
        block = main[device, local]
        imag = extra[device, pl.ds(local, 1), :]
        wide = []
        for axis in range(3):
            vector = block[3 + axis : 4 + axis]
            for part, current in enumerate((block[7:8], imag)):
                product = vector * current
                high = product.astype(BF16).astype(F32)
                row = 2 * axis + part
                weights[row : row + 1, :] = high
                weights[8 + row : 9 + row, :] = product - high
        return block

    def write_first(sign, points, radii):
        norm = jnp.sum(points * points, axis=0, keepdims=True) + radii * radii
        high, middle, low = split_three(points)
        for slot, piece in enumerate((high, high, middle, middle, high, low)):
            feat_first[sign, 3 * slot : 3 * slot + 3, :] = piece
        for row, piece in enumerate(split_three(norm)):
            feat_first[sign, 18 + row : 19 + row, :] = piece

    def write_second(sign, points, radii):
        norm = jnp.sum(points * points, axis=0, keepdims=True) + radii * radii
        high, middle, low = split_three(-2.0 * points)
        for slot, piece in enumerate((high, middle, high, middle, low, high)):
            feat_second[sign, 3 * slot : 3 * slot + 3, :] = piece
        for row, piece in enumerate(split_three(norm)):
            feat_second[sign, 21 + row : 22 + row, :] = piece

    def contract(sums, block, scale):
        both = sums[0:8] + sums[8:16]
        result = 0.0
        for axis in range(3):
            result = result + both[2 * axis : 2 * axis + 2] * block[3 + axis : 4 + axis]
        return result * scale

    def apply(signs, first, second, block_first, block_second, scale):
        for sign in range(signs):
            step = (gauss_step if sign else -gauss_step) if signs > 1 else 0.0
            for block, write in ((block_first, write_first), (block_second, write_second)):
                points = block[0:3] - 0.5
                if signs > 1:
                    points = points + step * block[3:6]
                write(sign, points, block[6:7])
        left = [feat_first[sign].T.astype(BF16) for sign in range(signs)]
        right = [feat_second[sign].astype(BF16) for sign in range(signs)]
        from_first = weight_first[...].astype(BF16)
        from_second = weight_second[...].astype(BF16)
        mirror = jnp.zeros((16, CS), F32)
        direct = []
        for start in range(0, CS, CHUNK):
            inverse = 0.0
            for one in left:
                for other in right:
                    inverse = inverse + lax.rsqrt(dot_nn(one[start : start + CHUNK], other))
            high = inverse.astype(BF16)
            low = (inverse - high.astype(F32)).astype(BF16)
            direct.append(dot_nt(from_second, high) + dot_nt(from_second, low))
            rows = from_first[:, start : start + CHUNK]
            mirror = mirror + dot_nn(rows, high) + dot_nn(rows, low)
        direct = jnp.concatenate(direct, 1)
        total[first] += contract(direct, block_first, scale)
        keep = jnp.where(first == second, 0.0, scale)
        total[second] += contract(mirror, block_second, keep)

    def visit(turn, now):
        flag = now % 4
        second = now // 4 % 1024
        first = now // 4096
        block_first = load(first, weight_first)
        block_second = load(second, weight_second)

        @pl.when(flag == 2)
        def _():
            apply(2, first, second, block_first, block_second, kernel_gain * 0.25)

        @pl.when(flag != 2)
        def _():
            apply(1, first, second, block_first, block_second, kernel_gain)

        return pick(turn + 1)

    lax.fori_loop(0, mine, visit, pick(0))


def pair_terms(main, extra):
    devices, clusters = main.shape[0], main.shape[1]
    return pl.pallas_call(
        pair_kernel,
        out_shape=jax.ShapeDtypeStruct((devices * clusters, 2, CS), F32),
        in_specs=[VMEM, VMEM],
        out_specs=VMEM,
        scratch_shapes=[
            pltpu.VMEM((2, 32, CS), F32),
            pltpu.VMEM((2, 32, CS), F32),
            pltpu.VMEM((16, CS), F32),
            pltpu.VMEM((16, CS), F32),
        ],
    )(main, extra)


def finish_kernel(owned, resist, cur, slot, out, stack):
    clusters = owned.shape[0]
    slots = slot[...]
    sums = jnp.zeros((16, slots.shape[1]), F32)
    stack[...] = jnp.zeros_like(stack)
    for cluster in range(clusters):
        for part, piece in enumerate(split_three(owned[cluster])):
            stack[2 * part : 2 * part + 2, :] = piece
        sums = sums + dot_nn(stack[...].astype(BF16), one_hot_rows(slots, cluster * CS, CS))
    induced = sums[0:2] + sums[2:4] + sums[4:6]
    scaled = resist[...] * cur[...]
    out[0:1, :] = scaled[0:1] - induced[1:2]
    out[1:2, :] = scaled[1:2] + induced[0:1]


def finish(owned, resist, currents, slot_of):
    return pl.pallas_call(
        finish_kernel,
        out_shape=jax.ShapeDtypeStruct(currents.shape, F32),
        in_specs=[VMEM] * 4,
        out_specs=VMEM,
        scratch_shapes=[pltpu.VMEM((16, CS), F32)],
    )(owned, resist[None, :], currents, slot_of[None, :])


def on_device(positions, segments, radius, currents, resist, slot_of, pair_list, near_flag):
    main, extra = order_elements(
        positions, segments, radius, currents, slot_of, pair_list, near_flag
    )
    main_all = lax.all_gather(main, ("row", "col"))
    extra_all = lax.all_gather(extra, ("row", "col"))
    total = pair_terms(main_all, extra_all)
    owned = lax.psum_scatter(total, ("row", "col"), scatter_dimension=0, tiled=True)
    return finish(owned, resist, currents, slot_of)


def solution(mesh):
    return jax.shard_map(
        on_device,
        mesh=mesh,
        in_specs=(
            P(None, ("row", "col")),
            P(None, ("row", "col")),
            P(("row", "col")),
            P(None, ("row", "col")),
            P(("row", "col")),
            P(("row", "col")),
            P(("row", "col"), None),
            P(("row", "col")),
        ),
        out_specs=P(None, ("row", "col")),
        check_vma=False,
    )
```

```python
import functools
import math

import jax
import jax.numpy as jnp
from jax import lax
from jax.experimental import pallas as pl
from jax.experimental.pallas import tpu as pltpu
from jax.sharding import PartitionSpec as P

CS = 512
F32 = jnp.float32
BF16 = jnp.bfloat16
MESH = pl.DeviceIdType.MESH
gauss_step = 0.5 / math.sqrt(3.0)
kernel_gain = 0.25
VMEM = pl.BlockSpec(memory_space=pltpu.VMEM)
CHUNK = 256


def split_three(value):
    high = value.astype(BF16).astype(F32)
    rest = value - high
    middle = rest.astype(BF16).astype(F32)
    return high, middle, rest - middle


def dot_nn(left, right):
    return lax.dot_general(left, right, (((1,), (0,)), ((), ())), preferred_element_type=F32)


def dot_nt(left, right):
    return lax.dot_general(left, right, (((1,), (1,)), ((), ())), preferred_element_type=F32)


def one_hot_rows(slots, start, count):
    rows = lax.broadcasted_iota(jnp.int32, (count, slots.shape[1]), 0) + start
    return jnp.where(rows == slots, 1.0, 0.0).astype(BF16)


def order_kernel(pos, seg, rad, cur, slot, pair, flag, main, extra, stack):
    clusters = main.shape[0]
    slots = slot[...]
    stack[...] = jnp.zeros_like(stack)
    for source, row in ((pos, 0), (seg, 3), (rad, 6), (cur, 7)):
        count = source.shape[0]
        for part, piece in enumerate(split_three(source[...])):
            stack[part * 16 + row : part * 16 + row + count, :] = piece
    parts = stack[...].astype(BF16)
    for cluster in range(clusters):
        sums = dot_nt(parts, one_hot_rows(slots, cluster * CS, CS))
        ordered = sums[0:16] + sums[16:32] + sums[32:48]
        main[cluster] = ordered[0:8]
        extra[cluster : cluster + 1, :] = ordered[8:9]
    listed = pair.shape[1]
    extra[clusters : clusters + 2, :] = jnp.zeros((2, CS), F32)
    extra[clusters : clusters + 1, 0:listed] = pair[0:1, :].astype(F32)
    extra[clusters : clusters + 1, 128 : 128 + listed] = pair[1:2, :].astype(F32)
    extra[clusters : clusters + 1, 256 : 256 + listed] = flag[...].astype(F32)


def order_elements(positions, segments, radius, currents, slot_of, pair_list, near_flag):
    local = positions.shape[1]
    clusters = local // CS
    return pl.pallas_call(
        order_kernel,
        out_shape=(
            jax.ShapeDtypeStruct((clusters, 8, CS), F32),
            jax.ShapeDtypeStruct((clusters + 2, CS), F32),
        ),
        in_specs=[VMEM] * 7,
        out_specs=(VMEM, VMEM),
        scratch_shapes=[pltpu.VMEM((48, local), F32)],
    )(
        positions,
        segments,
        radius[None, :],
        currents,
        slot_of[None, :],
        pair_list.T,
        near_flag[None, :],
    )


def pair_kernel(main, extra, total, feat_first, feat_second, weight_first, weight_second):
    devices, clusters = main.shape[0], main.shape[1]
    me = lax.axis_index("row") * lax.axis_size("col") + lax.axis_index("col")
    total[...] = jnp.zeros_like(total)
    for feat, ones in ((feat_first, 21), (feat_second, 18)):
        feat[...] = jnp.zeros_like(feat)
        for sign in range(2):
            feat[sign, ones : ones + 3, :] = jnp.ones((3, CS), F32)
    weight_first[...] = jnp.zeros_like(weight_first)
    weight_second[...] = jnp.zeros_like(weight_second)

    lists = extra[:, clusters, :]
    first_ids, second_ids, flags = lists[:, 0:128], lists[:, 128:256], lists[:, 256:384]
    code = (first_ids * 1024.0 + second_ids) * 4.0 + flags
    is_near = jnp.where(flags > 1.5, 1.0, 0.0)
    is_far = jnp.where(jnp.abs(flags - 1.0) < 0.5, 1.0, 0.0)
    before_lane = jnp.where(
        lax.broadcasted_iota(jnp.int32, (128, 128), 0) < lax.broadcasted_iota(jnp.int32, (128, 128), 1),
        1.0,
        0.0,
    ).astype(BF16)
    before_row = jnp.where(
        lax.broadcasted_iota(jnp.int32, (devices, devices), 1)
        < lax.broadcasted_iota(jnp.int32, (devices, devices), 0),
        1.0,
        0.0,
    ).astype(BF16)

    def rank_in(mask):
        in_row = dot_nn(mask.astype(BF16), before_lane)
        above = jnp.sum(dot_nn(before_row, mask.astype(BF16)), axis=1, keepdims=True)
        return in_row + above

    near_count = jnp.sum(is_near)
    live_count = near_count + jnp.sum(is_far)
    rank = jnp.where(
        is_near > 0.5,
        rank_in(is_near),
        jnp.where(is_far > 0.5, rank_in(is_far) + near_count, -1.0),
    ).astype(jnp.int32)
    mine = (live_count.astype(jnp.int32) + (devices - 1 - me)) // devices

    def pick(turn):
        found = jnp.where(rank == turn * devices + me, code, 0.0)
        return jnp.sum(found).astype(jnp.int32)

    def load(cluster, weights):
        device, local = cluster // clusters, cluster % clusters
        block = main[device, local]
        imag = extra[device, pl.ds(local, 1), :]
        wide = []
        for axis in range(3):
            vector = block[3 + axis : 4 + axis]
            for part, current in enumerate((block[7:8], imag)):
                product = vector * current
                high = product.astype(BF16).astype(F32)
                row = 2 * axis + part
                weights[row : row + 1, :] = high
                weights[8 + row : 9 + row, :] = product - high
        return block

    def write_first(sign, points, radii):
        norm = jnp.sum(points * points, axis=0, keepdims=True) + radii * radii
        high, middle, low = split_three(points)
        for slot, piece in enumerate((high, high, middle, middle, high, low)):
            feat_first[sign, 3 * slot : 3 * slot + 3, :] = piece
        for row, piece in enumerate(split_three(norm)):
            feat_first[sign, 18 + row : 19 + row, :] = piece

    def write_second(sign, points, radii):
        norm = jnp.sum(points * points, axis=0, keepdims=True) + radii * radii
        high, middle, low = split_three(-2.0 * points)
        for slot, piece in enumerate((high, middle, high, middle, low, high)):
            feat_second[sign, 3 * slot : 3 * slot + 3, :] = piece
        for row, piece in enumerate(split_three(norm)):
            feat_second[sign, 21 + row : 22 + row, :] = piece

    def contract(sums, block, scale):
        both = sums[0:8] + sums[8:16]
        result = 0.0
        for axis in range(3):
            result = result + both[2 * axis : 2 * axis + 2] * block[3 + axis : 4 + axis]
        return result * scale

    def apply(signs, first, second, block_first, block_second, scale):
        for sign in range(signs):
            step = (gauss_step if sign else -gauss_step) if signs > 1 else 0.0
            for block, write in ((block_first, write_first), (block_second, write_second)):
                points = block[0:3] - 0.5
                if signs > 1:
                    points = points + step * block[3:6]
                write(sign, points, block[6:7])
        left = [feat_first[sign].T.astype(BF16) for sign in range(signs)]
        right = [feat_second[sign].astype(BF16) for sign in range(signs)]
        from_first = weight_first[...].astype(BF16)
        from_second = weight_second[...].astype(BF16)
        mirror = jnp.zeros((16, CS), F32)
        direct = []
        for start in range(0, CS, CHUNK):
            inverse = 0.0
            for one in left:
                for other in right:
                    inverse = inverse + lax.rsqrt(dot_nn(one[start : start + CHUNK], other))
            high = inverse.astype(BF16)
            low = (inverse - high.astype(F32)).astype(BF16)
            direct.append(dot_nt(from_second, high) + dot_nt(from_second, low))
            rows = from_first[:, start : start + CHUNK]
            mirror = mirror + dot_nn(rows, high) + dot_nn(rows, low)
        direct = jnp.concatenate(direct, 1)
        total[first] += contract(direct, block_first, scale)
        keep = jnp.where(first == second, 0.0, scale)
        total[second] += contract(mirror, block_second, keep)

    def visit(turn, now):
        flag = now % 4
        second = now // 4 % 1024
        first = now // 4096
        block_first = load(first, weight_first)
        block_second = load(second, weight_second)

        @pl.when(flag == 2)
        def _():
            apply(2, first, second, block_first, block_second, kernel_gain * 0.25)

        @pl.when(flag != 2)
        def _():
            apply(1, first, second, block_first, block_second, kernel_gain)

        return pick(turn + 1)

    lax.fori_loop(0, mine, visit, pick(0))


def pair_terms(main, extra):
    devices, clusters = main.shape[0], main.shape[1]
    return pl.pallas_call(
        pair_kernel,
        out_shape=jax.ShapeDtypeStruct((devices * clusters, 2, CS), F32),
        in_specs=[VMEM, VMEM],
        out_specs=VMEM,
        scratch_shapes=[
            pltpu.VMEM((2, 32, CS), F32),
            pltpu.VMEM((2, 32, CS), F32),
            pltpu.VMEM((16, CS), F32),
            pltpu.VMEM((16, CS), F32),
        ],
    )(main, extra)


def finish_kernel(owned, resist, cur, slot, out, stack):
    clusters = owned.shape[0]
    slots = slot[...]
    sums = jnp.zeros((16, slots.shape[1]), F32)
    stack[...] = jnp.zeros_like(stack)
    for cluster in range(clusters):
        for part, piece in enumerate(split_three(owned[cluster])):
            stack[2 * part : 2 * part + 2, :] = piece
        sums = sums + dot_nn(stack[...].astype(BF16), one_hot_rows(slots, cluster * CS, CS))
    induced = sums[0:2] + sums[2:4] + sums[4:6]
    scaled = resist[...] * cur[...]
    out[0:1, :] = scaled[0:1] - induced[1:2]
    out[1:2, :] = scaled[1:2] + induced[0:1]


def finish(owned, resist, currents, slot_of):
    return pl.pallas_call(
        finish_kernel,
        out_shape=jax.ShapeDtypeStruct(currents.shape, F32),
        in_specs=[VMEM] * 4,
        out_specs=VMEM,
        scratch_shapes=[pltpu.VMEM((16, CS), F32)],
    )(owned, resist[None, :], currents, slot_of[None, :])


def greet(barrier, peers):
    for row, col in peers:
        pl.semaphore_signal(
            barrier, inc=1, device_id={"row": row, "col": col}, device_id_type=MESH
        )
    pl.semaphore_wait(barrier, len(peers))


def gather_kernel(main, extra, main_all, extra_all, send_sem, recv_sem, own_sem):
    row_count, col_count = lax.axis_size("row"), lax.axis_size("col")
    row, col = lax.axis_index("row"), lax.axis_index("col")
    me = row * col_count + col
    chips = row_count // 2
    other = row + 1 - 2 * lax.rem(row, 2)
    gathered = (main_all, extra_all)

    def row_at(base, step):
        return lax.rem(base + 2 * step, row_count)

    def col_at(step):
        return lax.rem(col + step, col_count)

    greet(
        pltpu.get_barrier_semaphore(),
        [(row, col_at(k)) for k in range(1, col_count)]
        + [(row_at(row, k), col) for k in range(1, chips)]
        + [(other, col)],
    )
    own = [
        pltpu.make_async_copy(source, target.at[me], own_sem.at[part])
        for part, (source, target) in enumerate(zip((main, extra), gathered))
    ]
    for copy in own:
        copy.start()

    def copies(origin, lane, to_row, to_col, mine=False):
        return [
            pltpu.make_async_remote_copy(
                src_ref=source if mine else target.at[origin],
                dst_ref=target.at[origin],
                send_sem=send_sem.at[part, lane],
                recv_sem=recv_sem.at[part, origin],
                device_id={"row": to_row, "col": to_col},
                device_id_type=MESH,
            )
            for part, (source, target) in enumerate(zip((main, extra), gathered))
        ]

    sent = []

    def push(origin, to_row, to_col, mine=False):
        started = copies(origin, len(sent), to_row, to_col, mine)
        for copy in started:
            copy.start()
        sent.append(started)

    def arrive(origin):
        for copy in copies(origin, 0, other, col):
            copy.wait_recv()

    def fan_out(origin, mine=False):
        for k in range(1, chips):
            push(origin, row_at(row, k), col, mine)
        push(origin, other, col, mine)

    for k in range(1, col_count):
        push(me, row, col_at(k), True)
    fan_out(me, True)
    for k in range(1, col_count):
        origin = row * col_count + col_at(col_count - k)
        arrive(origin)
        fan_out(origin)
    for block in range(col_count):
        for k in range(1, chips):
            origin = row_at(row, chips - k) * col_count + col_at(col_count - block)
            arrive(origin)
            push(origin, other, col)
    for block in range(col_count):
        for k in range(chips):
            arrive(row_at(other, chips - k) * col_count + col_at(col_count - block))
    for started in sent:
        for copy in started:
            copy.wait_send()
    for copy in own:
        copy.wait()


def gather_all(main, extra):
    row_count, col_count = lax.axis_size("row"), lax.axis_size("col")
    devices = row_count * col_count
    lanes = col_count - 1 + col_count * (row_count - 1)
    return pl.pallas_call(
        gather_kernel,
        out_shape=(
            jax.ShapeDtypeStruct((devices,) + main.shape, F32),
            jax.ShapeDtypeStruct((devices,) + extra.shape, F32),
        ),
        in_specs=[VMEM, VMEM],
        out_specs=(VMEM, VMEM),
        scratch_shapes=[
            pltpu.SemaphoreType.DMA((2, lanes)),
            pltpu.SemaphoreType.DMA((2, devices)),
            pltpu.SemaphoreType.DMA((2,)),
        ],
        compiler_params=pltpu.CompilerParams(collective_id=0, has_side_effects=True),
    )(main, extra)


def scatter_kernel(total, owned, arrived, send_sem, recv_sem):
    row_count, col_count = lax.axis_size("row"), lax.axis_size("col")
    devices = row_count * col_count
    clusters = owned.shape[0]
    me = lax.axis_index("row") * col_count + lax.axis_index("col")
    barrier = pltpu.get_barrier_semaphore()

    def call_on(step, _):
        peer = lax.rem(me + step, devices)
        pl.semaphore_signal(
            barrier,
            inc=1,
            device_id={"row": peer // col_count, "col": lax.rem(peer, col_count)},
            device_id_type=MESH,
        )
        return 0

    lax.fori_loop(1, devices, call_on, 0)
    pl.semaphore_wait(barrier, devices - 1)

    def copy_of(step):
        peer = lax.rem(me + step, devices)
        return pltpu.make_async_remote_copy(
            src_ref=total.at[pl.ds(peer * clusters, clusters)],
            dst_ref=arrived.at[step],
            send_sem=send_sem.at[step],
            recv_sem=recv_sem.at[step],
            device_id={"row": peer // col_count, "col": lax.rem(peer, col_count)},
            device_id_type=MESH,
        )

    def begin(step, _):
        copy_of(step).start()
        return 0

    lax.fori_loop(1, devices, begin, 0)
    owned[...] = total[pl.ds(me * clusters, clusters)]

    def collect(step, _):
        copy_of(step).wait_recv()
        owned[...] += arrived[step]
        return 0

    lax.fori_loop(1, devices, collect, 0)

    def end(step, _):
        copy_of(step).wait_send()
        return 0

    lax.fori_loop(1, devices, end, 0)


def scatter_sum(total, clusters):
    devices = lax.axis_size("row") * lax.axis_size("col")
    return pl.pallas_call(
        scatter_kernel,
        out_shape=jax.ShapeDtypeStruct((clusters,) + total.shape[1:], F32),
        in_specs=[VMEM],
        out_specs=VMEM,
        scratch_shapes=[
            pltpu.VMEM((devices, clusters) + total.shape[1:], F32),
            pltpu.SemaphoreType.DMA((devices,)),
            pltpu.SemaphoreType.DMA((devices,)),
        ],
        compiler_params=pltpu.CompilerParams(collective_id=1, has_side_effects=True),
    )(total)


def on_device(positions, segments, radius, currents, resist, slot_of, pair_list, near_flag):
    main, extra = order_elements(
        positions, segments, radius, currents, slot_of, pair_list, near_flag
    )
    main_all, extra_all = gather_all(main, extra)
    total = pair_terms(main_all, extra_all)
    owned = scatter_sum(total, main.shape[0])
    return finish(owned, resist, currents, slot_of)


def solution(mesh):
    return jax.shard_map(
        on_device,
        mesh=mesh,
        in_specs=(
            P(None, ("row", "col")),
            P(None, ("row", "col")),
            P(("row", "col")),
            P(None, ("row", "col")),
            P(("row", "col")),
            P(("row", "col")),
            P(("row", "col"), None),
            P(("row", "col")),
        ),
        out_specs=P(None, ("row", "col")),
        check_vma=False,
    )
```

```python
import functools
import math

import jax
import jax.numpy as jnp
from jax import lax
from jax.experimental import pallas as pl
from jax.experimental.pallas import tpu as pltpu
from jax.sharding import PartitionSpec as P

CS = 512
F32 = jnp.float32
BF16 = jnp.bfloat16
MESH = pl.DeviceIdType.MESH
gauss_step = 0.5 / math.sqrt(3.0)
kernel_gain = 0.25
VMEM = pl.BlockSpec(memory_space=pltpu.VMEM)
TALL = 256
WIDE = 512
FAR = 2


def split_three(value):
    high = value.astype(BF16).astype(F32)
    rest = value - high
    middle = rest.astype(BF16).astype(F32)
    return high, middle, rest - middle


def dot_nn(left, right):
    return lax.dot_general(left, right, (((1,), (0,)), ((), ())), preferred_element_type=F32)


def dot_nt(left, right):
    return lax.dot_general(left, right, (((1,), (1,)), ((), ())), preferred_element_type=F32)


def one_hot_rows(slots, start, count):
    rows = lax.broadcasted_iota(jnp.int32, (count, slots.shape[1]), 0) + start
    return jnp.where(rows == slots, 1.0, 0.0).astype(BF16)


def order_kernel(pos, seg, rad, cur, slot, pair, flag, main, extra, stack):
    clusters = main.shape[0]
    slots = slot[...]
    stack[...] = jnp.zeros_like(stack)
    for source, row in ((pos, 0), (seg, 3), (rad, 6), (cur, 7)):
        count = source.shape[0]
        for part, piece in enumerate(split_three(source[...])):
            stack[part * 16 + row : part * 16 + row + count, :] = piece
    parts = stack[...].astype(BF16)
    for cluster in range(clusters):
        sums = dot_nt(parts, one_hot_rows(slots, cluster * CS, CS))
        ordered = sums[0:16] + sums[16:32] + sums[32:48]
        main[cluster] = ordered[0:8]
        extra[cluster : cluster + 1, :] = ordered[8:9]
    listed = pair.shape[1]
    extra[clusters : clusters + 2, :] = jnp.zeros((2, CS), F32)
    extra[clusters : clusters + 1, 0:listed] = pair[0:1, :].astype(F32)
    extra[clusters : clusters + 1, 128 : 128 + listed] = pair[1:2, :].astype(F32)
    extra[clusters : clusters + 1, 256 : 256 + listed] = flag[...].astype(F32)


def order_elements(positions, segments, radius, currents, slot_of, pair_list, near_flag):
    local = positions.shape[1]
    clusters = local // CS
    return pl.pallas_call(
        order_kernel,
        out_shape=(
            jax.ShapeDtypeStruct((clusters, 8, CS), F32),
            jax.ShapeDtypeStruct((clusters + 2, CS), F32),
        ),
        in_specs=[VMEM] * 7,
        out_specs=(VMEM, VMEM),
        scratch_shapes=[pltpu.VMEM((48, local), F32)],
    )(
        positions,
        segments,
        radius[None, :],
        currents,
        slot_of[None, :],
        pair_list.T,
        near_flag[None, :],
    )


def pair_kernel(main, extra, total, feat_first, feat_second, weight_first, weight_second):
    devices, clusters = main.shape[0], main.shape[1]
    me = lax.axis_index("row") * lax.axis_size("col") + lax.axis_index("col")
    total[...] = jnp.zeros_like(total)
    for feat, ones in ((feat_first, 21), (feat_second, 18)):
        feat[...] = jnp.zeros_like(feat)
        for unit in range(FAR):
            for sign in range(2):
                feat[unit, sign, ones : ones + 3, :] = jnp.ones((3, CS), F32)
    weight_first[...] = jnp.zeros_like(weight_first)
    weight_second[...] = jnp.zeros_like(weight_second)

    lists = extra[:, clusters, :]
    first_ids, second_ids, flags = lists[:, 0:128], lists[:, 128:256], lists[:, 256:384]
    code = (first_ids * 1024.0 + second_ids) * 4.0 + flags
    is_near = jnp.where(flags > 1.5, 1.0, 0.0)
    is_far = jnp.where(jnp.abs(flags - 1.0) < 0.5, 1.0, 0.0)
    before_lane = jnp.where(
        lax.broadcasted_iota(jnp.int32, (128, 128), 0) < lax.broadcasted_iota(jnp.int32, (128, 128), 1),
        1.0,
        0.0,
    ).astype(BF16)
    before_row = jnp.where(
        lax.broadcasted_iota(jnp.int32, (devices, devices), 1)
        < lax.broadcasted_iota(jnp.int32, (devices, devices), 0),
        1.0,
        0.0,
    ).astype(BF16)

    def rank_in(mask):
        in_row = dot_nn(mask.astype(BF16), before_lane)
        above = jnp.sum(dot_nn(before_row, mask.astype(BF16)), axis=1, keepdims=True)
        return in_row + above

    near_count = jnp.sum(is_near)
    live_count = near_count + jnp.sum(is_far)
    rank = jnp.where(
        is_near > 0.5,
        rank_in(is_near),
        jnp.where(is_far > 0.5, rank_in(is_far) + near_count, -1.0),
    ).astype(jnp.int32)
    def share(count):
        return (count.astype(jnp.int32) + (devices - 1 - me)) // devices

    mine_near, mine = share(near_count), share(live_count)

    def pick(turn):
        found = jnp.where(rank == turn * devices + me, code, 0.0)
        return jnp.sum(found).astype(jnp.int32)

    def load(cluster, weights):
        device, local = cluster // clusters, cluster % clusters
        block = main[device, local]
        imag = extra[device, pl.ds(local, 1), :]
        for axis in range(3):
            vector = block[3 + axis : 4 + axis]
            for part, current in enumerate((block[7:8], imag)):
                product = vector * current
                high = product.astype(BF16).astype(F32)
                row = 2 * axis + part
                weights[row : row + 1, :] = high
                weights[8 + row : 9 + row, :] = product - high
        return block

    def write(feat, points, radii, gain, order, norm_row):
        norm = jnp.sum(points * points, axis=0, keepdims=True) + radii * radii
        parts = split_three(gain * points)
        for slot, part in enumerate(order):
            feat[3 * slot : 3 * slot + 3, :] = parts[part]
        for row, piece in enumerate(split_three(norm)):
            feat[norm_row + row : norm_row + row + 1, :] = piece

    def contract(sums, block, scale):
        both = sums[0:8] + sums[8:16]
        result = 0.0
        for axis in range(3):
            result = result + both[2 * axis : 2 * axis + 2] * block[3 + axis : 4 + axis]
        return result * scale

    def apply(codes_and_scales, signs):
        units = []
        for unit, (now, scale) in enumerate(codes_and_scales):
            first, second = now // 4096, now // 4 % 1024
            block_first = load(first, weight_first.at[unit])
            block_second = load(second, weight_second.at[unit])
            for sign in range(signs):
                step = gauss_step if sign else -gauss_step
                for block, feat, gain, order, norm_row in (
                    (block_first, feat_first, 1.0, (0, 0, 1, 1, 0, 2), 18),
                    (block_second, feat_second, -2.0, (0, 1, 0, 1, 2, 0), 21),
                ):
                    points = block[0:3] - 0.5
                    if signs > 1:
                        points = points + step * block[3:6]
                    write(feat.at[unit, sign], points, block[6:7], gain, order, norm_row)
            units.append((unit, first, second, block_first, block_second, scale))
        sides = []
        for unit, *_ in units:
            left = [feat_first[unit, sign].T.astype(BF16) for sign in range(signs)]
            right = [feat_second[unit, sign].astype(BF16) for sign in range(signs)]
            from_first = weight_first[unit].astype(BF16)
            turned = weight_second[unit].T.astype(BF16)
            sides.append((left, right, from_first, turned))
        mirrors = [[0.0 for _ in range(0, CS, WIDE)] for _ in units]
        directs = [[] for _ in units]
        for start in range(0, CS, TALL):
            sums = [0.0 for _ in units]
            for index, across in enumerate(range(0, CS, WIDE)):
                for unit, (left, right, from_first, turned) in enumerate(sides):
                    inverse = 0.0
                    for one in left:
                        for other in right:
                            inverse = inverse + lax.rsqrt(
                                dot_nn(one[start : start + TALL], other[:, across : across + WIDE])
                            )
                    high = inverse.astype(BF16)
                    low = (inverse - high.astype(F32)).astype(BF16)
                    near_side = turned[across : across + WIDE]
                    rows = from_first[:, start : start + TALL]
                    sums[unit] = sums[unit] + dot_nn(high, near_side) + dot_nn(low, near_side)
                    mirrors[unit][index] = (
                        mirrors[unit][index] + dot_nn(rows, high) + dot_nn(rows, low)
                    )
            for unit, _ in enumerate(units):
                directs[unit].append(sums[unit])
        terms = []
        for unit, first, second, block_first, block_second, scale in units:
            direct = jnp.concatenate(directs[unit], 0).T
            mirror = jnp.concatenate(mirrors[unit], 1)
            keep = jnp.where(first == second, 0.0, scale)
            terms.append((first, contract(direct, block_first, scale)))
            terms.append((second, contract(mirror, block_second, keep)))
        for cluster, term in terms:
            total[cluster] += term

    def visit_near(turn, now):
        apply([(now, kernel_gain * 0.25)], 2)
        return pick(turn + 1)

    def visit_far(step, codes):
        turn = mine_near + FAR * step
        apply(
            [
                (now, kernel_gain if unit == 0 else jnp.where(turn + unit < mine, kernel_gain, 0.0))
                for unit, now in enumerate(codes)
            ],
            1,
        )
        return tuple(pick(turn + FAR + unit) for unit in range(FAR))

    start = lax.fori_loop(0, mine_near, visit_near, pick(0))
    lax.fori_loop(
        0,
        (mine - mine_near + FAR - 1) // FAR,
        visit_far,
        (start,) + tuple(pick(mine_near + unit) for unit in range(1, FAR)),
    )


def pair_terms(main, extra):
    devices, clusters = main.shape[0], main.shape[1]
    return pl.pallas_call(
        pair_kernel,
        out_shape=jax.ShapeDtypeStruct((devices * clusters, 2, CS), F32),
        in_specs=[VMEM, VMEM],
        out_specs=VMEM,
        scratch_shapes=[
            pltpu.VMEM((FAR, 2, 32, CS), F32),
            pltpu.VMEM((FAR, 2, 32, CS), F32),
            pltpu.VMEM((FAR, 16, CS), F32),
            pltpu.VMEM((FAR, 16, CS), F32),
        ],
    )(main, extra)


def finish_kernel(owned, resist, cur, slot, out, stack):
    clusters = owned.shape[0]
    slots = slot[...]
    sums = jnp.zeros((16, slots.shape[1]), F32)
    stack[...] = jnp.zeros_like(stack)
    for cluster in range(clusters):
        for part, piece in enumerate(split_three(owned[cluster])):
            stack[2 * part : 2 * part + 2, :] = piece
        sums = sums + dot_nn(stack[...].astype(BF16), one_hot_rows(slots, cluster * CS, CS))
    induced = sums[0:2] + sums[2:4] + sums[4:6]
    scaled = resist[...] * cur[...]
    out[0:1, :] = scaled[0:1] - induced[1:2]
    out[1:2, :] = scaled[1:2] + induced[0:1]


def finish(owned, resist, currents, slot_of):
    return pl.pallas_call(
        finish_kernel,
        out_shape=jax.ShapeDtypeStruct(currents.shape, F32),
        in_specs=[VMEM] * 4,
        out_specs=VMEM,
        scratch_shapes=[pltpu.VMEM((16, CS), F32)],
    )(owned, resist[None, :], currents, slot_of[None, :])


def greet(barrier, peers):
    for row, col in peers:
        pl.semaphore_signal(
            barrier, inc=1, device_id={"row": row, "col": col}, device_id_type=MESH
        )
    pl.semaphore_wait(barrier, len(peers))


def gather_kernel(main, extra, main_all, extra_all, send_sem, recv_sem, own_sem):
    row_count, col_count = lax.axis_size("row"), lax.axis_size("col")
    row, col = lax.axis_index("row"), lax.axis_index("col")
    me = row * col_count + col
    chips = row_count // 2
    other = row + 1 - 2 * lax.rem(row, 2)
    gathered = (main_all, extra_all)

    def row_at(base, step):
        return lax.rem(base + 2 * step, row_count)

    def col_at(step):
        return lax.rem(col + step, col_count)

    greet(
        pltpu.get_barrier_semaphore(),
        [(row, col_at(k)) for k in range(1, col_count)]
        + [(row_at(row, k), col) for k in range(1, chips)]
        + [(other, col)],
    )
    own = [
        pltpu.make_async_copy(source, target.at[me], own_sem.at[part])
        for part, (source, target) in enumerate(zip((main, extra), gathered))
    ]
    for copy in own:
        copy.start()

    def copies(origin, lane, to_row, to_col, mine=False):
        return [
            pltpu.make_async_remote_copy(
                src_ref=source if mine else target.at[origin],
                dst_ref=target.at[origin],
                send_sem=send_sem.at[part, lane],
                recv_sem=recv_sem.at[part, origin],
                device_id={"row": to_row, "col": to_col},
                device_id_type=MESH,
            )
            for part, (source, target) in enumerate(zip((main, extra), gathered))
        ]

    sent = []

    def push(origin, to_row, to_col, mine=False):
        started = copies(origin, len(sent), to_row, to_col, mine)
        for copy in started:
            copy.start()
        sent.append(started)

    def arrive(origin):
        for copy in copies(origin, 0, other, col):
            copy.wait_recv()

    def fan_out(origin, mine=False):
        for k in range(1, chips):
            push(origin, row_at(row, k), col, mine)
        push(origin, other, col, mine)

    for k in range(1, col_count):
        push(me, row, col_at(k), True)
    fan_out(me, True)
    for k in range(1, col_count):
        origin = row * col_count + col_at(col_count - k)
        arrive(origin)
        fan_out(origin)
    for block in range(col_count):
        for k in range(1, chips):
            origin = row_at(row, chips - k) * col_count + col_at(col_count - block)
            arrive(origin)
            push(origin, other, col)
    for block in range(col_count):
        for k in range(chips):
            arrive(row_at(other, chips - k) * col_count + col_at(col_count - block))
    for started in sent:
        for copy in started:
            copy.wait_send()
    for copy in own:
        copy.wait()


def gather_all(main, extra):
    row_count, col_count = lax.axis_size("row"), lax.axis_size("col")
    devices = row_count * col_count
    lanes = col_count - 1 + col_count * (row_count - 1)
    return pl.pallas_call(
        gather_kernel,
        out_shape=(
            jax.ShapeDtypeStruct((devices,) + main.shape, F32),
            jax.ShapeDtypeStruct((devices,) + extra.shape, F32),
        ),
        in_specs=[VMEM, VMEM],
        out_specs=(VMEM, VMEM),
        scratch_shapes=[
            pltpu.SemaphoreType.DMA((2, lanes)),
            pltpu.SemaphoreType.DMA((2, devices)),
            pltpu.SemaphoreType.DMA((2,)),
        ],
        compiler_params=pltpu.CompilerParams(collective_id=0, has_side_effects=True),
    )(main, extra)


def scatter_kernel(total, owned, arrived, send_sem, recv_sem):
    row_count, col_count = lax.axis_size("row"), lax.axis_size("col")
    devices = row_count * col_count
    clusters = owned.shape[0]
    me = lax.axis_index("row") * col_count + lax.axis_index("col")
    barrier = pltpu.get_barrier_semaphore()

    def call_on(step, _):
        peer = lax.rem(me + step, devices)
        pl.semaphore_signal(
            barrier,
            inc=1,
            device_id={"row": peer // col_count, "col": lax.rem(peer, col_count)},
            device_id_type=MESH,
        )
        return 0

    lax.fori_loop(1, devices, call_on, 0)
    pl.semaphore_wait(barrier, devices - 1)

    def copy_of(step):
        peer = lax.rem(me + step, devices)
        return pltpu.make_async_remote_copy(
            src_ref=total.at[pl.ds(peer * clusters, clusters)],
            dst_ref=arrived.at[step],
            send_sem=send_sem.at[step],
            recv_sem=recv_sem.at[step],
            device_id={"row": peer // col_count, "col": lax.rem(peer, col_count)},
            device_id_type=MESH,
        )

    def begin(step, _):
        copy_of(step).start()
        return 0

    lax.fori_loop(1, devices, begin, 0)
    owned[...] = total[pl.ds(me * clusters, clusters)]

    def collect(step, _):
        copy_of(step).wait_recv()
        owned[...] += arrived[step]
        return 0

    lax.fori_loop(1, devices, collect, 0)

    def end(step, _):
        copy_of(step).wait_send()
        return 0

    lax.fori_loop(1, devices, end, 0)


def scatter_sum(total, clusters):
    devices = lax.axis_size("row") * lax.axis_size("col")
    return pl.pallas_call(
        scatter_kernel,
        out_shape=jax.ShapeDtypeStruct((clusters,) + total.shape[1:], F32),
        in_specs=[VMEM],
        out_specs=VMEM,
        scratch_shapes=[
            pltpu.VMEM((devices, clusters) + total.shape[1:], F32),
            pltpu.SemaphoreType.DMA((devices,)),
            pltpu.SemaphoreType.DMA((devices,)),
        ],
        compiler_params=pltpu.CompilerParams(collective_id=1, has_side_effects=True),
    )(total)


def on_device(positions, segments, radius, currents, resist, slot_of, pair_list, near_flag):
    main, extra = order_elements(
        positions, segments, radius, currents, slot_of, pair_list, near_flag
    )
    main_all, extra_all = gather_all(main, extra)
    total = pair_terms(main_all, extra_all)
    owned = scatter_sum(total, main.shape[0])
    return finish(owned, resist, currents, slot_of)


def solution(mesh):
    return jax.shard_map(
        on_device,
        mesh=mesh,
        in_specs=(
            P(None, ("row", "col")),
            P(None, ("row", "col")),
            P(("row", "col")),
            P(None, ("row", "col")),
            P(("row", "col")),
            P(("row", "col")),
            P(("row", "col"), None),
            P(("row", "col")),
        ),
        out_specs=P(None, ("row", "col")),
        check_vma=False,
    )
```

```python
import functools
import math

import jax
import jax.numpy as jnp
from jax import lax
from jax.experimental import pallas as pl
from jax.experimental.pallas import tpu as pltpu
from jax.sharding import PartitionSpec as P

CS = 512
F32 = jnp.float32
BF16 = jnp.bfloat16
MESH = pl.DeviceIdType.MESH
gauss_step = 0.5 / math.sqrt(3.0)
kernel_gain = 0.25
VMEM = pl.BlockSpec(memory_space=pltpu.VMEM)
TALL = 256
WIDE = 512
FAR = 2


def split_three(value):
    high = value.astype(BF16).astype(F32)
    rest = value - high
    middle = rest.astype(BF16).astype(F32)
    return high, middle, rest - middle


def dot_nn(left, right):
    return lax.dot_general(left, right, (((1,), (0,)), ((), ())), preferred_element_type=F32)


def dot_nt(left, right):
    return lax.dot_general(left, right, (((1,), (1,)), ((), ())), preferred_element_type=F32)


def one_hot_rows(slots, start, count):
    rows = lax.broadcasted_iota(jnp.int32, (count, slots.shape[1]), 0) + start
    return jnp.where(rows == slots, 1.0, 0.0).astype(BF16)


def order_into(pos, seg, rad, cur, slot, pair, flag, main, extra, stack):
    clusters = main.shape[0]
    slots = slot[...]
    stack[...] = jnp.zeros_like(stack)
    for source, row in ((pos, 0), (seg, 3), (rad, 6), (cur, 7)):
        count = source.shape[0]
        for part, piece in enumerate(split_three(source[...])):
            stack[part * 16 + row : part * 16 + row + count, :] = piece
    parts = stack[...].astype(BF16)
    for cluster in range(clusters):
        sums = dot_nt(parts, one_hot_rows(slots, cluster * CS, CS))
        ordered = sums[0:16] + sums[16:32] + sums[32:48]
        main[cluster] = ordered[0:8]
        extra[cluster : cluster + 1, :] = ordered[8:9]
    listed = pair.shape[1]
    extra[clusters : clusters + 2, :] = jnp.zeros((2, CS), F32)
    extra[clusters : clusters + 1, 0:listed] = pair[0:1, :].astype(F32)
    extra[clusters : clusters + 1, 128 : 128 + listed] = pair[1:2, :].astype(F32)
    extra[clusters : clusters + 1, 256 : 256 + listed] = flag[...].astype(F32)


def pair_kernel(main, extra, total, feat_first, feat_second, weight_first, weight_second):
    devices, clusters = main.shape[0], main.shape[1]
    me = lax.axis_index("row") * lax.axis_size("col") + lax.axis_index("col")
    total[...] = jnp.zeros_like(total)
    for feat, ones in ((feat_first, 21), (feat_second, 18)):
        feat[...] = jnp.zeros_like(feat)
        for unit in range(FAR):
            for sign in range(2):
                feat[unit, sign, ones : ones + 3, :] = jnp.ones((3, CS), F32)
    weight_first[...] = jnp.zeros_like(weight_first)
    weight_second[...] = jnp.zeros_like(weight_second)

    lists = extra[:, clusters, :]
    first_ids, second_ids, flags = lists[:, 0:128], lists[:, 128:256], lists[:, 256:384]
    code = (first_ids * 1024.0 + second_ids) * 4.0 + flags
    is_near = jnp.where(flags > 1.5, 1.0, 0.0)
    is_far = jnp.where(jnp.abs(flags - 1.0) < 0.5, 1.0, 0.0)
    before_lane = jnp.where(
        lax.broadcasted_iota(jnp.int32, (128, 128), 0) < lax.broadcasted_iota(jnp.int32, (128, 128), 1),
        1.0,
        0.0,
    ).astype(BF16)
    before_row = jnp.where(
        lax.broadcasted_iota(jnp.int32, (devices, devices), 1)
        < lax.broadcasted_iota(jnp.int32, (devices, devices), 0),
        1.0,
        0.0,
    ).astype(BF16)

    def rank_in(mask):
        in_row = dot_nn(mask.astype(BF16), before_lane)
        above = jnp.sum(dot_nn(before_row, mask.astype(BF16)), axis=1, keepdims=True)
        return in_row + above

    near_count = jnp.sum(is_near)
    live_count = near_count + jnp.sum(is_far)
    rank = jnp.where(
        is_near > 0.5,
        rank_in(is_near),
        jnp.where(is_far > 0.5, rank_in(is_far) + near_count, -1.0),
    ).astype(jnp.int32)
    def share(count):
        return (count.astype(jnp.int32) + (devices - 1 - me)) // devices

    mine_near, mine = share(near_count), share(live_count)

    def pick(turn):
        found = jnp.where(rank == turn * devices + me, code, 0.0)
        return jnp.sum(found).astype(jnp.int32)

    def load(cluster, weights):
        device, local = cluster // clusters, cluster % clusters
        block = main[device, local]
        imag = extra[device, pl.ds(local, 1), :]
        for axis in range(3):
            vector = block[3 + axis : 4 + axis]
            for part, current in enumerate((block[7:8], imag)):
                product = vector * current
                high = product.astype(BF16).astype(F32)
                row = 2 * axis + part
                weights[row : row + 1, :] = high
                weights[8 + row : 9 + row, :] = product - high
        return block

    def write(feat, points, radii, gain, order, norm_row):
        norm = jnp.sum(points * points, axis=0, keepdims=True) + radii * radii
        parts = split_three(gain * points)
        for slot, part in enumerate(order):
            feat[3 * slot : 3 * slot + 3, :] = parts[part]
        for row, piece in enumerate(split_three(norm)):
            feat[norm_row + row : norm_row + row + 1, :] = piece

    def contract(sums, block, scale):
        both = sums[0:8] + sums[8:16]
        result = 0.0
        for axis in range(3):
            result = result + both[2 * axis : 2 * axis + 2] * block[3 + axis : 4 + axis]
        return result * scale

    def apply(codes_and_scales, signs):
        units = []
        for unit, (now, scale) in enumerate(codes_and_scales):
            first, second = now // 4096, now // 4 % 1024
            block_first = load(first, weight_first.at[unit])
            block_second = load(second, weight_second.at[unit])
            for sign in range(signs):
                step = gauss_step if sign else -gauss_step
                for block, feat, gain, order, norm_row in (
                    (block_first, feat_first, 1.0, (0, 0, 1, 1, 0, 2), 18),
                    (block_second, feat_second, -2.0, (0, 1, 0, 1, 2, 0), 21),
                ):
                    points = block[0:3] - 0.5
                    if signs > 1:
                        points = points + step * block[3:6]
                    write(feat.at[unit, sign], points, block[6:7], gain, order, norm_row)
            units.append((unit, first, second, block_first, block_second, scale))
        sides = []
        for unit, *_ in units:
            left = [feat_first[unit, sign].T.astype(BF16) for sign in range(signs)]
            right = [feat_second[unit, sign].astype(BF16) for sign in range(signs)]
            from_first = weight_first[unit].astype(BF16)
            turned = weight_second[unit].T.astype(BF16)
            sides.append((left, right, from_first, turned))
        mirrors = [[0.0 for _ in range(0, CS, WIDE)] for _ in units]
        directs = [[] for _ in units]
        for start in range(0, CS, TALL):
            sums = [0.0 for _ in units]
            for index, across in enumerate(range(0, CS, WIDE)):
                for unit, (left, right, from_first, turned) in enumerate(sides):
                    inverse = 0.0
                    for one in left:
                        for other in right:
                            inverse = inverse + lax.rsqrt(
                                dot_nn(one[start : start + TALL], other[:, across : across + WIDE])
                            )
                    high = inverse.astype(BF16)
                    low = (inverse - high.astype(F32)).astype(BF16)
                    near_side = turned[across : across + WIDE]
                    rows = from_first[:, start : start + TALL]
                    sums[unit] = sums[unit] + dot_nn(high, near_side) + dot_nn(low, near_side)
                    mirrors[unit][index] = (
                        mirrors[unit][index] + dot_nn(rows, high) + dot_nn(rows, low)
                    )
            for unit, _ in enumerate(units):
                directs[unit].append(sums[unit])
        terms = []
        for unit, first, second, block_first, block_second, scale in units:
            direct = jnp.concatenate(directs[unit], 0).T
            mirror = jnp.concatenate(mirrors[unit], 1)
            keep = jnp.where(first == second, 0.0, scale)
            terms.append((first, contract(direct, block_first, scale)))
            terms.append((second, contract(mirror, block_second, keep)))
        for cluster, term in terms:
            total[cluster] += term

    def visit_near(turn, now):
        apply([(now, kernel_gain * 0.25)], 2)
        return pick(turn + 1)

    def visit_far(step, codes):
        turn = mine_near + FAR * step
        apply(
            [
                (now, kernel_gain if unit == 0 else jnp.where(turn + unit < mine, kernel_gain, 0.0))
                for unit, now in enumerate(codes)
            ],
            1,
        )
        return tuple(pick(turn + FAR + unit) for unit in range(FAR))

    start = lax.fori_loop(0, mine_near, visit_near, pick(0))
    lax.fori_loop(
        0,
        (mine - mine_near + FAR - 1) // FAR,
        visit_far,
        (start,) + tuple(pick(mine_near + unit) for unit in range(1, FAR)),
    )


def pair_terms(main, extra):
    devices, clusters = main.shape[0], main.shape[1]
    return pl.pallas_call(
        pair_kernel,
        out_shape=jax.ShapeDtypeStruct((devices * clusters, 2, CS), F32),
        in_specs=[VMEM, VMEM],
        out_specs=VMEM,
        scratch_shapes=[
            pltpu.VMEM((FAR, 2, 32, CS), F32),
            pltpu.VMEM((FAR, 2, 32, CS), F32),
            pltpu.VMEM((FAR, 16, CS), F32),
            pltpu.VMEM((FAR, 16, CS), F32),
        ],
    )(main, extra)


def gather_kernel(
    pos, seg, rad, cur, slot, pair, flag, main_all, extra_all, stack, send_sem, recv_sem
):
    row_count, col_count = lax.axis_size("row"), lax.axis_size("col")
    row, col = lax.axis_index("row"), lax.axis_index("col")
    me = row * col_count + col
    chips = row_count // 2
    other = row + 1 - 2 * lax.rem(row, 2)
    gathered = (main_all, extra_all)

    def row_at(base, step):
        return lax.rem(base + 2 * step, row_count)

    def col_at(step):
        return lax.rem(col + step, col_count)

    barrier = pltpu.get_barrier_semaphore()
    peers = [(row, col_at(k)) for k in range(1, col_count)]
    peers += [(row_at(row, k), col) for k in range(1, chips)] + [(other, col)]
    for to_row, to_col in peers:
        pl.semaphore_signal(
            barrier, inc=1, device_id={"row": to_row, "col": to_col}, device_id_type=MESH
        )
    order_into(
        pos, seg, rad, cur, slot, pair, flag, main_all.at[me], extra_all.at[me], stack
    )
    pl.semaphore_wait(barrier, len(peers))

    def copies(origin, lane, to_row, to_col):
        return [
            pltpu.make_async_remote_copy(
                src_ref=target.at[origin],
                dst_ref=target.at[origin],
                send_sem=send_sem.at[part, lane],
                recv_sem=recv_sem.at[part, origin],
                device_id={"row": to_row, "col": to_col},
                device_id_type=MESH,
            )
            for part, target in enumerate(gathered)
        ]

    sent = []

    def push(origin, to_row, to_col):
        started = copies(origin, len(sent), to_row, to_col)
        for copy in started:
            copy.start()
        sent.append(started)

    def arrive(origin):
        for copy in copies(origin, 0, other, col):
            copy.wait_recv()

    def fan_out(origin):
        for k in range(1, chips):
            push(origin, row_at(row, k), col)
        push(origin, other, col)

    for k in range(1, col_count):
        push(me, row, col_at(k))
    fan_out(me)
    for k in range(1, col_count):
        origin = row * col_count + col_at(col_count - k)
        arrive(origin)
        fan_out(origin)
    for block in range(col_count):
        for k in range(1, chips):
            origin = row_at(row, chips - k) * col_count + col_at(col_count - block)
            arrive(origin)
            push(origin, other, col)
    for block in range(col_count):
        for k in range(chips):
            arrive(row_at(other, chips - k) * col_count + col_at(col_count - block))
    for started in sent:
        for copy in started:
            copy.wait_send()


def gather_all(positions, segments, radius, currents, slot_of, pair_list, near_flag):
    row_count, col_count = lax.axis_size("row"), lax.axis_size("col")
    devices = row_count * col_count
    local = positions.shape[1]
    clusters = local // CS
    lanes = col_count - 1 + col_count * (row_count - 1)
    return pl.pallas_call(
        gather_kernel,
        out_shape=(
            jax.ShapeDtypeStruct((devices, clusters, 8, CS), F32),
            jax.ShapeDtypeStruct((devices, clusters + 2, CS), F32),
        ),
        in_specs=[VMEM] * 7,
        out_specs=(VMEM, VMEM),
        scratch_shapes=[
            pltpu.VMEM((48, local), F32),
            pltpu.SemaphoreType.DMA((2, lanes)),
            pltpu.SemaphoreType.DMA((2, devices)),
        ],
        compiler_params=pltpu.CompilerParams(collective_id=0, has_side_effects=True),
    )(
        positions,
        segments,
        radius[None, :],
        currents,
        slot_of[None, :],
        pair_list.T,
        near_flag[None, :],
    )


def scatter_kernel(
    total, resist, cur, slot, out, owned, arrived, chosen, stack, send_sem, recv_sem
):
    row_count, col_count = lax.axis_size("row"), lax.axis_size("col")
    devices = row_count * col_count
    clusters = owned.shape[0]
    me = lax.axis_index("row") * col_count + lax.axis_index("col")
    barrier = pltpu.get_barrier_semaphore()

    def call_on(step, _):
        peer = lax.rem(me + step, devices)
        pl.semaphore_signal(
            barrier,
            inc=1,
            device_id={"row": peer // col_count, "col": lax.rem(peer, col_count)},
            device_id_type=MESH,
        )
        return 0

    lax.fori_loop(1, devices, call_on, 0)
    slots = slot[...]
    for cluster in range(clusters):
        chosen[cluster] = one_hot_rows(slots, cluster * CS, CS)
    stack[...] = jnp.zeros_like(stack)
    pl.semaphore_wait(barrier, devices - 1)

    def copy_of(step):
        peer = lax.rem(me + step, devices)
        return pltpu.make_async_remote_copy(
            src_ref=total.at[pl.ds(peer * clusters, clusters)],
            dst_ref=arrived.at[step],
            send_sem=send_sem.at[step],
            recv_sem=recv_sem.at[step],
            device_id={"row": peer // col_count, "col": lax.rem(peer, col_count)},
            device_id_type=MESH,
        )

    def begin(step, _):
        copy_of(step).start()
        return 0

    lax.fori_loop(1, devices, begin, 0)
    owned[...] = total[pl.ds(me * clusters, clusters)]

    def collect(step, _):
        copy_of(step).wait_recv()
        owned[...] += arrived[step]
        return 0

    lax.fori_loop(1, devices, collect, 0)
    sums = jnp.zeros((16, slots.shape[1]), F32)
    for cluster in range(clusters):
        for part, piece in enumerate(split_three(owned[cluster])):
            stack[2 * part : 2 * part + 2, :] = piece
        sums = sums + dot_nn(stack[...].astype(BF16), chosen[cluster])
    induced = sums[0:2] + sums[2:4] + sums[4:6]
    scaled = resist[...] * cur[...]
    out[0:1, :] = scaled[0:1] - induced[1:2]
    out[1:2, :] = scaled[1:2] + induced[0:1]

    def end(step, _):
        copy_of(step).wait_send()
        return 0

    lax.fori_loop(1, devices, end, 0)


def scatter_finish(total, resist, currents, slot_of):
    devices = lax.axis_size("row") * lax.axis_size("col")
    local = currents.shape[1]
    clusters = local // CS
    return pl.pallas_call(
        scatter_kernel,
        out_shape=jax.ShapeDtypeStruct(currents.shape, F32),
        in_specs=[VMEM] * 4,
        out_specs=VMEM,
        scratch_shapes=[
            pltpu.VMEM((clusters,) + total.shape[1:], F32),
            pltpu.VMEM((devices, clusters) + total.shape[1:], F32),
            pltpu.VMEM((clusters, CS, local), BF16),
            pltpu.VMEM((16, CS), F32),
            pltpu.SemaphoreType.DMA((devices,)),
            pltpu.SemaphoreType.DMA((devices,)),
        ],
        compiler_params=pltpu.CompilerParams(collective_id=1, has_side_effects=True),
    )(total, resist[None, :], currents, slot_of[None, :])


def on_device(positions, segments, radius, currents, resist, slot_of, pair_list, near_flag):
    main_all, extra_all = gather_all(
        positions, segments, radius, currents, slot_of, pair_list, near_flag
    )
    total = pair_terms(main_all, extra_all)
    return scatter_finish(total, resist, currents, slot_of)


def solution(mesh):
    return jax.shard_map(
        on_device,
        mesh=mesh,
        in_specs=(
            P(None, ("row", "col")),
            P(None, ("row", "col")),
            P(("row", "col")),
            P(None, ("row", "col")),
            P(("row", "col")),
            P(("row", "col")),
            P(("row", "col"), None),
            P(("row", "col")),
        ),
        out_specs=P(None, ("row", "col")),
        check_vma=False,
    )
```
